32 devices in a mesh: groups: 2 (over x), seq: 8 (over z, y), head: 2 (over core).
Axes of the slice: x: 2, y: 2, z: 4, core: 2. Of those that a mesh axis runs over, the one named last changes fastest.
Arguments:
- queries: bfloat16 [8192, 2048], P(('groups', 'seq'), 'head'), parts along dimension 0, may hold values from -6 to 6
- keys: bfloat16 [8192, 1024], P(('groups', 'seq'), 'head'), parts along dimension 0, may hold values from -6 to 6
- values: bfloat16 [8192, 1024], P(('groups', 'seq'), 'head'), parts along dimension 0, may hold values from -6 to 6
- segments: int32 [8192], P('groups'), parts along dimension 0, may hold values from 0 to 7, never falling along the last dimension, each value on 1 to 1024 neighbouring positions
- out_weight: bfloat16 [2048, 5376], P('head'), may hold values from -0.125 to 0.125
Outputs:
- mixed: bfloat16 [8192, 5376], P(('groups', 'seq')), parts along dimension 0
The draws below stay inside these ranges and needn't reach their ends.
There are 2 independent parts, one for each index of `groups`. The reference program is written for one: setup_inputs(seed, part) draws one part's arguments, and reference() takes and returns one part's arrays. A program takes and returns all parts, laid end to end along the dimension named above; an argument that names none is the same for every part. Nothing has to cross between parts.
Inputs may be any that keep to these rules, and one draw needn't show every extreme that they name: `segments`: document ids never fall along the slab; each document has 1 to 1024 tokens, one exactly 1024.
All inputs are finite; a program needn't handle non-finite values.
Results may differ from the reference program's by a relative error of at most 0.011.
Values may be sent and summed in bfloat16 or wider, within the bound.
A program may use at most 128 MiB of HBM per device.

```python
import math
import jax
import jax.numpy as jnp
import numpy as np
from jax import lax

D = 5376
QUERY_HEADS = 16
KEY_VALUE_HEADS = 8
HEAD_SIZE = 128
SCALAR = 168
ATTENTION_SPAN = 1024
SLAB_TOKENS = 4096


def draw_keys(key, part):
    final_output = jnp.clip(jax.random.normal(jax.random.fold_in(key, 11), (SLAB_TOKENS, KEY_VALUE_HEADS * HEAD_SIZE), jnp.float32), -6.0, 6.0)
    return final_output.astype(jnp.bfloat16)


def draw_queries(key, part):
    final_output = jnp.clip(jax.random.normal(jax.random.fold_in(key, 21), (SLAB_TOKENS, QUERY_HEADS * HEAD_SIZE), jnp.float32), -6.0, 6.0)
    return final_output.astype(jnp.bfloat16)


def shard_levels(rng, extent, pieces, least, largest):
    def one(position, parts):
        steps = jax.random.uniform(jax.random.fold_in(jax.random.fold_in(rng, 6), position), (parts,), jnp.float32, least / len(pieces), largest / len(pieces))
        return jnp.repeat(jnp.exp(steps), extent[position] // parts).reshape((-1,) + (1,) * (len(extent) - position - 1))

    loudness = one(*pieces[0])
    for cut in pieces[1:]:
        loudness = loudness * one(*cut)
    return loudness


def profile(amount, total, limit, skew):
    loads = [(1 << 20) // math.isqrt(rank ** skew) + 1 for rank in range(2, amount + 1)]
    rest, holding = total - limit - (amount - 1), [1] * (amount - 1)
    while rest > 0:
        candidates = [i for i in range(amount - 1) if holding[i] < limit]
        mass, remaining = sum([loads[i] for i in candidates]), rest
        for i in candidates:
            extra = min(limit - holding[i], max(1, remaining * loads[i] // mass), rest)
            holding[i] = holding[i] + extra
            rest = rest - extra
    return np.array([limit] + holding)


def uneven_parts(key, amount, total, reach, skew):
    if amount == 2:
        one = jax.random.randint(key, (), max(1, total - reach), min(reach, total - 1) + 1)
        return jnp.stack([one, total - one])
    sizes = jnp.asarray(profile(amount, total, reach, skew), jnp.int32)
    pairs = (amount - 1) // 2
    giver, receiver = sizes[1:1 + 2 * pairs:2], sizes[2:2 + 2 * pairs:2]
    margin = jnp.minimum(giver - 1, reach - receiver)
    passed = jax.random.randint(jax.random.fold_in(key, 1), (pairs,), 0, 1 << 20) % (margin + 1)
    sizes = sizes.at[1:1 + 2 * pairs:2].set(giver - passed).at[2:2 + 2 * pairs:2].set(receiver + passed)
    return sizes[jax.random.permutation(jax.random.fold_in(key, 2), amount)]


def noise(own_key, shape, width, reach, cuts=(), held_as=jnp.bfloat16):
    loudness = shard_levels(own_key, shape, cuts, -0.22, 0.18) if cuts else 1.0
    array = jax.random.normal(own_key, shape, jnp.float32) * width * loudness
    return jnp.minimum(jnp.maximum(array, -reach), reach).astype(held_as)


def setup_inputs(seed: int = 0, part: int = 0) -> dict:
    seeds = jax.random.split(jax.random.key(seed), 6)
    part_splits = jax.random.split(jax.random.fold_in(seeds[5], part), 6)
    queries = draw_queries(jax.random.fold_in(jax.random.fold_in(seeds[5], part), 71), part)
    keys = draw_keys(jax.random.fold_in(jax.random.fold_in(seeds[5], part), 71), part)
    values = noise(part_splits[2], (SLAB_TOKENS, KEY_VALUE_HEADS * HEAD_SIZE), 1.0, 6.0, ((0, 8), (1, 2)))
    segments = jnp.searchsorted(jnp.cumsum(uneven_parts(part_splits[3], 8, SLAB_TOKENS, SLAB_TOKENS // 4, 2)), jnp.arange(SLAB_TOKENS), side="right").astype(jnp.int32)
    out_weight = noise(seeds[4], (QUERY_HEADS * HEAD_SIZE, D), (QUERY_HEADS * HEAD_SIZE) ** -0.5, 0.125, ((0, 2),))
    return {"queries": queries, "keys": keys, "values": values, "segments": segments, "out_weight": out_weight}


def reference(queries, keys, values, segments, out_weight):
    query_group = QUERY_HEADS // KEY_VALUE_HEADS
    token_block = math.gcd(SLAB_TOKENS, 512)
    window_span = ATTENTION_SPAN + token_block
    padded_keys = jnp.concatenate([jnp.zeros((ATTENTION_SPAN, KEY_VALUE_HEADS * HEAD_SIZE), keys.dtype), keys])
    padded_values = jnp.concatenate([jnp.zeros((ATTENTION_SPAN, KEY_VALUE_HEADS * HEAD_SIZE), values.dtype), values])
    pad_segments = jnp.concatenate([jnp.full((ATTENTION_SPAN,), -1, jnp.int32), segments.astype(jnp.int32)])

    def one_block(block_id):
        first_index = (block_id * token_block).astype(jnp.int32)
        query_matrix_rows = lax.dynamic_slice_in_dim(queries, first_index, token_block, 0).astype(jnp.float32).reshape(token_block, KEY_VALUE_HEADS, query_group, HEAD_SIZE)
        key_matrix_rows = lax.dynamic_slice_in_dim(padded_keys, first_index, window_span, 0).astype(jnp.float32).reshape(window_span, KEY_VALUE_HEADS, HEAD_SIZE)
        value_matrix_rows = lax.dynamic_slice_in_dim(padded_values, first_index, window_span, 0).astype(jnp.float32).reshape(window_span, KEY_VALUE_HEADS, HEAD_SIZE)
        seg_query = lax.dynamic_slice_in_dim(segments.astype(jnp.int32), first_index, token_block, 0)
        seg_key = lax.dynamic_slice_in_dim(pad_segments, first_index, window_span, 0)
        query_pos = first_index + jnp.arange(token_block, dtype=jnp.int32)
        key_pos = first_index - ATTENTION_SPAN + jnp.arange(window_span, dtype=jnp.int32)
        allowed = (key_pos[None, :] <= query_pos[:, None]) & (query_pos[:, None] - key_pos[None, :] < ATTENTION_SPAN) & (seg_key[None, :] == seg_query[:, None])
        scores = jnp.einsum('qkgd,pkd->kgqp', query_matrix_rows, key_matrix_rows) * (SCALAR ** -0.5)
        masked = jnp.where(allowed, scores, -1e30)
        row_max = jnp.max(masked, axis=-1, keepdims=True)
        expo = jnp.where(allowed, jnp.exp(masked - row_max), 0.0)
        weights = (expo / jnp.sum(expo, axis=-1, keepdims=True)).astype(jnp.bfloat16)
        heads_out = jnp.einsum('kgqp,pkd->qkgd', weights.astype(jnp.float32), value_matrix_rows)
        return heads_out.astype(jnp.bfloat16).reshape(token_block, QUERY_HEADS * HEAD_SIZE)

    attended = lax.map(one_block, jnp.arange(SLAB_TOKENS // token_block, dtype=jnp.int32)).reshape(SLAB_TOKENS, QUERY_HEADS * HEAD_SIZE)
    return jnp.dot(attended, out_weight, preferred_element_type=jnp.float32).astype(jnp.bfloat16)
```

```python
import functools

import jax
import jax.numpy as jnp
from jax import lax
from jax.experimental import pallas as pl
from jax.experimental.pallas import tpu as pltpu
from jax.sharding import PartitionSpec as P

HEAD_SIZE = 128
SCALAR = 168
ATTENTION_SPAN = 1024
LOG2E = 1.4426950408889634
QUERY_TILE = 256
MESH = pl.DeviceIdType.MESH


def column_chunks(width):
    step = 768
    return [(at, min(step, width - at)) for at in range(0, width, step)]


def kernel(
    q_hbm, k_hbm, v_hbm, seg_ref, w_hbm, out_hbm,
    q_s, k_s, v_s, w_own, w_peer, att_own, att_peer, acc, stage, bias,
    q_sem, kv_sem, w_sem, ws_sem, wr_sem, zs_sem, zr_sem, ys_sem, yr_sem,
    as_sem, ar_sem, ol_sem, os_sem, or_sem,
):
    heads = k_s.shape[0]
    group = q_s.shape[0] // heads
    rows = q_s.shape[1]
    half = w_own.shape[1]
    seq = lax.axis_index("seq")
    core = lax.axis_index("head")
    peers = lax.axis_size("seq")
    odd = lax.rem(seq, 2)
    pair = seq + 1 - 2 * odd
    other = 1 - core
    chunks = column_chunks(half)

    def local_kv(which, h):
        src, dst = ((k_hbm, k_s), (v_hbm, v_s))[which]
        return pltpu.make_async_copy(
            src.at[:, pl.ds(h * HEAD_SIZE, HEAD_SIZE)],
            dst.at[h, pl.ds(2 * rows, rows), :], kv_sem.at[which, h])

    def local_q(n):
        return pltpu.make_async_copy(
            q_hbm.at[:, pl.ds(n * HEAD_SIZE, HEAD_SIZE)], q_s.at[n], q_sem.at[n])

    def far(which, h):
        src, dst = ((k_hbm, k_s), (v_hbm, v_s))[which]
        return pltpu.make_async_remote_copy(
            src_ref=src.at[:, pl.ds(h * HEAD_SIZE, HEAD_SIZE)],
            dst_ref=dst.at[h, pl.ds(0, rows), :],
            send_sem=zs_sem.at[which, h], recv_sem=zr_sem.at[which, h],
            device_id={"seq": seq + 2}, device_id_type=MESH)

    def near(which, h):
        src, dst = ((k_hbm, k_s), (v_hbm, v_s))[which]
        return pltpu.make_async_remote_copy(
            src_ref=src.at[:, pl.ds(h * HEAD_SIZE, HEAD_SIZE)],
            dst_ref=dst.at[h, pl.ds(rows, rows), :],
            send_sem=ys_sem.at[which, h], recv_sem=yr_sem.at[which, h],
            device_id={"seq": pair}, device_id_type=MESH)

    def relay(which, h):
        dst = (k_s, v_s)[which]
        return pltpu.make_async_remote_copy(
            src_ref=dst.at[h, pl.ds(0, rows), :],
            dst_ref=dst.at[h, pl.ds(rows, rows), :],
            send_sem=ys_sem.at[which, h], recv_sem=yr_sem.at[which, h],
            device_id={"seq": pair}, device_id_type=MESH)

    def weight_send():
        return pltpu.make_async_remote_copy(
            src_ref=w_hbm.at[:, pl.ds(pl.multiple_of(other * half, HEAD_SIZE), half)],
            dst_ref=w_peer, send_sem=ws_sem, recv_sem=wr_sem,
            device_id={"head": other}, device_id_type=MESH)

    def weight_local():
        return pltpu.make_async_copy(
            w_hbm.at[:, pl.ds(pl.multiple_of(core * half, HEAD_SIZE), half)], w_own, w_sem)

    def attended_send(h):
        return pltpu.make_async_remote_copy(
            src_ref=att_own.at[h], dst_ref=att_peer.at[h],
            send_sem=as_sem.at[h], recv_sem=ar_sem.at[h],
            device_id={"head": other}, device_id_type=MESH)

    def out_view(at, width, owner):
        return out_hbm.at[:, pl.ds(pl.multiple_of(owner * half + at, HEAD_SIZE), width)]

    def out_local(n):
        at, width = chunks[n]
        return pltpu.make_async_copy(
            stage.at[:, pl.ds(at, width)], out_view(at, width, core), ol_sem.at[n])

    def out_send(n):
        at, width = chunks[n]
        return pltpu.make_async_remote_copy(
            src_ref=stage.at[:, pl.ds(at, width)], dst_ref=out_view(at, width, core),
            send_sem=os_sem.at[n], recv_sem=or_sem.at[n],
            device_id={"head": other}, device_id_type=MESH)

    has_up = seq + 2 < peers
    has_down = seq >= 2
    even = odd == 0
    sends_near = jnp.logical_or(even, seq >= 3)
    relays = jnp.logical_and(jnp.logical_not(even), seq >= 3)
    gets_near = seq >= 1

    barrier = pltpu.get_barrier_semaphore()
    pl.semaphore_signal(barrier, inc=1, device_id={"head": other}, device_id_type=MESH)
    pl.semaphore_signal(barrier, inc=1, device_id={"seq": pair}, device_id_type=MESH)

    @pl.when(has_up)
    def _():
        pl.semaphore_signal(barrier, inc=1, device_id={"seq": seq + 2}, device_id_type=MESH)

    @pl.when(has_down)
    def _():
        pl.semaphore_signal(barrier, inc=1, device_id={"seq": seq - 2}, device_id_type=MESH)

    pl.semaphore_wait(
        barrier, 2 + jnp.minimum(peers - 1 - seq, 2) // 2 + jnp.minimum(seq, 2) // 2)

    for h in range(heads):
        for which in range(2):
            @pl.when(has_up)
            def _():
                far(which, h).start()

            @pl.when(even)
            def _():
                near(which, h).start()

    for h in range(heads):
        for which in range(2):
            local_kv(which, h).start()
        for g in range(group):
            local_q(h * group + g).start()
    weight_send().start()
    weight_local().start()

    @pl.when(jnp.logical_not(has_down))
    def _():
        k_s[:, 0:rows, :] = jnp.zeros((heads, rows, HEAD_SIZE), k_s.dtype)
        v_s[:, 0:rows, :] = jnp.zeros((heads, rows, HEAD_SIZE), v_s.dtype)

    @pl.when(jnp.logical_not(gets_near))
    def _():
        k_s[:, rows:2 * rows, :] = jnp.zeros((heads, rows, HEAD_SIZE), k_s.dtype)
        v_s[:, rows:2 * rows, :] = jnp.zeros((heads, rows, HEAD_SIZE), v_s.dtype)

    tile = QUERY_TILE
    span = ATTENTION_SPAN + tile
    seg_own = seg_ref[seq]
    seg_all = jnp.concatenate(
        [seg_ref[jnp.maximum(seq - 2, 0)], seg_ref[jnp.maximum(seq - 1, 0)], seg_own], axis=1)
    for b in range(rows // tile):
        seg_key = seg_all[:, b * tile:b * tile + span]
        for part in range(tile // 128):
            lo = b * tile + part * 128
            seg_query = jnp.broadcast_to(
                seg_own[:, lo:lo + 128].astype(jnp.float32), (128, 128)).T[:, :1]
            r = part * 128 + lax.broadcasted_iota(jnp.int32, (128, span), 0)
            c = lax.broadcasted_iota(jnp.int32, (128, span), 1)
            position = seq * rows - ATTENTION_SPAN + b * tile + c
            allowed = (
                (c <= r + ATTENTION_SPAN) & (c > r) & (position >= 0)
                & (seg_key.astype(jnp.float32) == seg_query)
            )
            bias[b, part * 128:(part + 1) * 128, :] = jnp.where(allowed, 0.0, -1e30)

    factor = SCALAR ** (-0.5) * LOG2E
    ones = jnp.ones((span, HEAD_SIZE), jnp.bfloat16)

    def product(first, last, at, width):
        own = jnp.concatenate([att_own[n] for n in range(first, last)], axis=1)
        far_side = jnp.concatenate([att_peer[n] for n in range(first, last)], axis=1)
        top = slice(first * group * HEAD_SIZE, last * group * HEAD_SIZE)
        cols = slice(at, at + width)
        return jnp.dot(own, w_own[top, cols], preferred_element_type=jnp.float32) + jnp.dot(
            far_side, w_peer[top, cols], preferred_element_type=jnp.float32)

    def step(h, carry):
        @pl.when(h == heads - 1)
        def _():
            weight_local().wait()
            weight_send().wait_recv()
            for n in range(heads - 1):
                attended_send(n).wait_recv()
            for at, width in chunks:
                acc[:, at:at + width] = product(0, heads - 1, at, width)

        for which in range(2):
            @pl.when(has_down)
            def _():
                far(which, h).wait_recv()

            @pl.when(relays)
            def _():
                relay(which, h).start()

        for which in range(2):
            local_kv(which, h).wait()

            @pl.when(gets_near)
            def _():
                near(which, h).wait_recv()
        for g in range(group):
            local_q(h * group + g).wait()
        for b in range(rows // tile):
            key = k_s[h, b * tile:b * tile + span, :]
            value = jnp.concatenate([v_s[h, b * tile:b * tile + span, :], ones], axis=1)
            for g in range(group):
                query = q_s[h * group + g, b * tile:(b + 1) * tile, :]
                scores = lax.dot_general(
                    query, key, (((1,), (1,)), ((), ())), preferred_element_type=jnp.float32)
                scores = scores + bias[b]
                top = jnp.max(scores, axis=1, keepdims=True)
                weights = jnp.exp2((scores - top) * factor).astype(jnp.bfloat16)
                mix = jnp.dot(weights, value, preferred_element_type=jnp.float32)
                att_own[h, b * tile:(b + 1) * tile, g * HEAD_SIZE:(g + 1) * HEAD_SIZE] = (
                    mix[:, :HEAD_SIZE] / mix[:, HEAD_SIZE:]).astype(jnp.bfloat16)
        attended_send(h).start()
        return carry

    lax.fori_loop(0, heads, step, 0)

    attended_send(heads - 1).wait_recv()
    for n, (at, width) in enumerate(chunks):
        stage[:, at:at + width] = (
            acc[:, at:at + width] + product(heads - 1, heads, at, width)).astype(jnp.bfloat16)
        out_local(n).start()
        out_send(n).start()

    for h in range(heads):
        attended_send(h).wait_send()
        for which in range(2):
            @pl.when(has_up)
            def _():
                far(which, h).wait_send()

            @pl.when(sends_near)
            def _():
                near(which, h).wait_send()
    weight_send().wait_send()
    for n in range(len(chunks)):
        out_local(n).wait()
        out_send(n).wait()


def shards(queries, keys, values, segments, out_weight):
    rows = queries.shape[0]
    assert 2 * rows == ATTENTION_SPAN
    heads = keys.shape[1] // HEAD_SIZE
    query_heads = queries.shape[1] // HEAD_SIZE
    group = query_heads // heads
    width = out_weight.shape[1]
    half = width // 2
    pieces = len(column_chunks(half))
    seg = segments.reshape(segments.shape[0] // rows, 1, rows)
    dma = pltpu.SemaphoreType.DMA
    anywhere = pl.BlockSpec(memory_space=pl.ANY)
    bf16 = jnp.bfloat16
    span = ATTENTION_SPAN + QUERY_TILE
    return pl.pallas_call(
        kernel,
        out_shape=jax.ShapeDtypeStruct((rows, width), bf16),
        in_specs=[anywhere, anywhere, anywhere, pl.BlockSpec(memory_space=pltpu.VMEM), anywhere],
        out_specs=anywhere,
        scratch_shapes=[
            pltpu.VMEM((query_heads, rows, HEAD_SIZE), bf16),
            pltpu.VMEM((heads, 3 * rows, HEAD_SIZE), bf16),
            pltpu.VMEM((heads, 3 * rows, HEAD_SIZE), bf16),
            pltpu.VMEM((out_weight.shape[0], half), bf16),
            pltpu.VMEM((out_weight.shape[0], half), bf16),
            pltpu.VMEM((heads, rows, group * HEAD_SIZE), bf16),
            pltpu.VMEM((heads, rows, group * HEAD_SIZE), bf16),
            pltpu.VMEM((rows, half), jnp.float32),
            pltpu.VMEM((rows, half), bf16),
            pltpu.VMEM((rows // QUERY_TILE, QUERY_TILE, span), jnp.float32),
            dma((query_heads,)), dma((2, heads)), dma, dma, dma,
            dma((2, heads)), dma((2, heads)), dma((2, heads)), dma((2, heads)),
            dma((heads,)), dma((heads,)), dma((pieces,)), dma((pieces,)), dma((pieces,)),
        ],
        compiler_params=pltpu.CompilerParams(
            collective_id=0, has_side_effects=True, vmem_limit_bytes=56 * 1024 * 1024),
    )(queries, keys, values, seg, out_weight)


def solution(mesh):
    placed = (
        P(("groups", "seq"), "head"),
        P(("groups", "seq"), "head"),
        P(("groups", "seq"), "head"),
        P("groups"),
        P("head", None),
    )
    return jax.shard_map(
        shards, mesh=mesh, in_specs=placed, out_specs=P(("groups", "seq"), None), check_vma=False
    )
```

```python
import functools

import jax
import jax.numpy as jnp
from jax import lax
from jax.experimental import pallas as pl
from jax.experimental.pallas import tpu as pltpu
from jax.sharding import PartitionSpec as P

HEAD_SIZE = 128
SCALAR = 168
ATTENTION_SPAN = 1024
LOG2E = 1.4426950408889634
QUERY_TILE = 256
MESH = pl.DeviceIdType.MESH


def column_chunks(width):
    step = 768
    return [(at, min(step, width - at)) for at in range(0, width, step)]


def kernel(
    q_hbm, k_hbm, v_hbm, seg_ref, w_hbm, out_ref,
    q_s, k_s, v_s, w_own, w_peer, att_own, att_peer, acc, part, part_top, bias,
    q_sem, kv_sem, w_sem, ws_sem, wr_sem, zs_sem, zr_sem, ys_sem, yr_sem,
    as_sem, ar_sem, os_sem, or_sem,
):
    heads = k_s.shape[0]
    group = q_s.shape[0] // heads
    rows = q_s.shape[1]
    half = w_own.shape[1]
    seq = lax.axis_index("seq")
    core = lax.axis_index("head")
    peers = lax.axis_size("seq")
    odd = lax.rem(seq, 2)
    pair = seq + 1 - 2 * odd
    other = 1 - core
    chunks = column_chunks(half)

    def local_kv(which, h):
        src, dst = ((k_hbm, k_s), (v_hbm, v_s))[which]
        return pltpu.make_async_copy(
            src.at[:, pl.ds(h * HEAD_SIZE, HEAD_SIZE)],
            dst.at[h, pl.ds(2 * rows, rows), :], kv_sem.at[which, h])

    def local_q(n):
        return pltpu.make_async_copy(
            q_hbm.at[:, pl.ds(n * HEAD_SIZE, HEAD_SIZE)], q_s.at[n], q_sem.at[n])

    def far(which, h):
        src, dst = ((k_hbm, k_s), (v_hbm, v_s))[which]
        return pltpu.make_async_remote_copy(
            src_ref=src.at[:, pl.ds(h * HEAD_SIZE, HEAD_SIZE)],
            dst_ref=dst.at[h, pl.ds(0, rows), :],
            send_sem=zs_sem.at[which, h], recv_sem=zr_sem.at[which, h],
            device_id={"seq": seq + 2}, device_id_type=MESH)

    def near(which, h):
        src, dst = ((k_hbm, k_s), (v_hbm, v_s))[which]
        return pltpu.make_async_remote_copy(
            src_ref=src.at[:, pl.ds(h * HEAD_SIZE, HEAD_SIZE)],
            dst_ref=dst.at[h, pl.ds(rows, rows), :],
            send_sem=ys_sem.at[which, h], recv_sem=yr_sem.at[which, h],
            device_id={"seq": pair}, device_id_type=MESH)

    def relay(which, h):
        dst = (k_s, v_s)[which]
        return pltpu.make_async_remote_copy(
            src_ref=dst.at[h, pl.ds(0, rows), :],
            dst_ref=dst.at[h, pl.ds(rows, rows), :],
            send_sem=ys_sem.at[which, h], recv_sem=yr_sem.at[which, h],
            device_id={"seq": pair}, device_id_type=MESH)

    def weight_send():
        return pltpu.make_async_remote_copy(
            src_ref=w_hbm.at[:, pl.ds(pl.multiple_of(other * half, HEAD_SIZE), half)],
            dst_ref=w_peer, send_sem=ws_sem, recv_sem=wr_sem,
            device_id={"head": other}, device_id_type=MESH)

    def weight_local():
        return pltpu.make_async_copy(
            w_hbm.at[:, pl.ds(pl.multiple_of(core * half, HEAD_SIZE), half)], w_own, w_sem)

    def attended_send(h):
        return pltpu.make_async_remote_copy(
            src_ref=att_own.at[h], dst_ref=att_peer.at[h],
            send_sem=as_sem.at[h], recv_sem=ar_sem.at[h],
            device_id={"head": other}, device_id_type=MESH)

    def out_view(n):
        at, width = chunks[n]
        return out_ref.at[:, pl.ds(pl.multiple_of(core * half + at, HEAD_SIZE), width)]

    def out_send(n):
        return pltpu.make_async_remote_copy(
            src_ref=out_view(n), dst_ref=out_view(n),
            send_sem=os_sem.at[n], recv_sem=or_sem.at[n],
            device_id={"head": other}, device_id_type=MESH)

    has_up = seq + 2 < peers
    has_down = seq >= 2
    even = odd == 0
    sends_near = jnp.logical_or(even, seq >= 3)
    relays = jnp.logical_and(jnp.logical_not(even), seq >= 3)
    gets_near = seq >= 1

    barrier = pltpu.get_barrier_semaphore()
    pl.semaphore_signal(barrier, inc=1, device_id={"head": other}, device_id_type=MESH)
    pl.semaphore_signal(barrier, inc=1, device_id={"seq": pair}, device_id_type=MESH)

    @pl.when(has_up)
    def _():
        pl.semaphore_signal(barrier, inc=1, device_id={"seq": seq + 2}, device_id_type=MESH)

    @pl.when(has_down)
    def _():
        pl.semaphore_signal(barrier, inc=1, device_id={"seq": seq - 2}, device_id_type=MESH)

    pl.semaphore_wait(
        barrier, 2 + jnp.minimum(peers - 1 - seq, 2) // 2 + jnp.minimum(seq, 2) // 2)

    for h in range(heads):
        for which in range(2):
            @pl.when(has_up)
            def _():
                far(which, h).start()

            @pl.when(even)
            def _():
                near(which, h).start()

    for h in range(heads):
        for which in range(2):
            local_kv(which, h).start()
        for g in range(group):
            local_q(h * group + g).start()
    weight_send().start()
    weight_local().start()

    @pl.when(jnp.logical_not(has_down))
    def _():
        k_s[:, 0:rows, :] = jnp.zeros((heads, rows, HEAD_SIZE), k_s.dtype)
        v_s[:, 0:rows, :] = jnp.zeros((heads, rows, HEAD_SIZE), v_s.dtype)

    @pl.when(jnp.logical_not(gets_near))
    def _():
        k_s[:, rows:2 * rows, :] = jnp.zeros((heads, rows, HEAD_SIZE), k_s.dtype)
        v_s[:, rows:2 * rows, :] = jnp.zeros((heads, rows, HEAD_SIZE), v_s.dtype)

    tile = QUERY_TILE
    span = ATTENTION_SPAN + tile
    seg_own = seg_ref[seq]
    seg_all = jnp.concatenate(
        [seg_ref[jnp.maximum(seq - 2, 0)], seg_ref[jnp.maximum(seq - 1, 0)], seg_own], axis=1)
    for b in range(rows // tile):
        seg_key = seg_all[:, b * tile:b * tile + span]
        for piece in range(tile // 128):
            lo = b * tile + piece * 128
            seg_query = jnp.broadcast_to(
                seg_own[:, lo:lo + 128].astype(jnp.float32), (128, 128)).T[:, :1]
            r = piece * 128 + lax.broadcasted_iota(jnp.int32, (128, span), 0)
            c = lax.broadcasted_iota(jnp.int32, (128, span), 1)
            position = seq * rows - ATTENTION_SPAN + b * tile + c
            allowed = (
                (c <= r + ATTENTION_SPAN) & (c > r) & (position >= 0)
                & (seg_key.astype(jnp.float32) == seg_query)
            )
            bias[b, piece * 128:(piece + 1) * 128, :] = jnp.where(allowed, 0.0, -1e30)

    factor = SCALAR ** (-0.5) * LOG2E
    halo = 2 * rows

    def with_ones(value):
        return jnp.concatenate([value, jnp.ones(value.shape, value.dtype)], axis=1)

    def score(query, key, added):
        return lax.dot_general(
            query, key, (((1,), (1,)), ((), ())), preferred_element_type=jnp.float32) + added

    def product(h, at, width):
        top = pl.ds(pl.multiple_of(h * (group * HEAD_SIZE), group * HEAD_SIZE), group * HEAD_SIZE)
        left = jnp.concatenate([att_own[h], att_peer[h]], axis=1)
        right = jnp.concatenate(
            [w_own[top, at:at + width], w_peer[top, at:at + width]], axis=0)
        return jnp.dot(left, right, preferred_element_type=jnp.float32)

    def inner_step(h, carry):
        for which in range(2):
            local_kv(which, h).wait()
        for g in range(group):
            local_q(h * group + g).wait()
        for b in range(rows // tile):
            inside = (b + 1) * tile
            key = k_s[h, halo:halo + inside, :]
            value = with_ones(v_s[h, halo:halo + inside, :])
            for g in range(group):
                n = h * group + g
                scores = score(
                    q_s[n, b * tile:(b + 1) * tile, :], key, bias[b, :, halo - b * tile:])
                top = jnp.max(scores, axis=1, keepdims=True)
                weights = jnp.exp2((scores - top) * factor).astype(jnp.bfloat16)
                part[n, b * tile:(b + 1) * tile, :] = jnp.dot(
                    weights, value, preferred_element_type=jnp.float32)
                part_top[n, b * tile:(b + 1) * tile, :] = jnp.broadcast_to(
                    top, (tile, HEAD_SIZE))
        return carry

    lax.fori_loop(0, heads, inner_step, 0)
    acc[...] = jnp.zeros_like(acc)

    def step(h, carry):
        for which in range(2):
            @pl.when(has_down)
            def _():
                far(which, h).wait_recv()

            @pl.when(relays)
            def _():
                relay(which, h).start()

        @pl.when(h == 1)
        def _():
            weight_local().wait()
            weight_send().wait_recv()

        @pl.when(h >= 1)
        def _():
            attended_send(h - 1).wait_recv()
            for at, width in chunks:
                acc[:, at:at + width] += product(h - 1, at, width)

        for which in range(2):
            @pl.when(gets_near)
            def _():
                near(which, h).wait_recv()

        for b in range(rows // tile):
            key = k_s[h, b * tile:halo, :]
            value = with_ones(v_s[h, b * tile:halo, :])
            for g in range(group):
                n = h * group + g
                scores = score(
                    q_s[n, b * tile:(b + 1) * tile, :], key, bias[b, :, :halo - b * tile])
                before = part_top[n, b * tile:(b + 1) * tile, :]
                top = jnp.maximum(jnp.max(scores, axis=1, keepdims=True), before[:, :1])
                weights = jnp.exp2((scores - top) * factor).astype(jnp.bfloat16)
                faded = jnp.exp2((before - top) * factor)
                mix = part[n, b * tile:(b + 1) * tile, :] * jnp.concatenate(
                    [faded, faded], axis=1) + jnp.dot(
                        weights, value, preferred_element_type=jnp.float32)
                att_own[h, b * tile:(b + 1) * tile, g * HEAD_SIZE:(g + 1) * HEAD_SIZE] = (
                    mix[:, :HEAD_SIZE] / mix[:, HEAD_SIZE:]).astype(jnp.bfloat16)
        attended_send(h).start()
        return carry

    lax.fori_loop(0, heads, step, 0)

    attended_send(heads - 1).wait_recv()
    for n, (at, width) in enumerate(chunks):
        out_view(n)[...] = (
            acc[:, at:at + width] + product(heads - 1, at, width)).astype(jnp.bfloat16)
        out_send(n).start()

    for h in range(heads):
        attended_send(h).wait_send()
        for which in range(2):
            @pl.when(has_up)
            def _():
                far(which, h).wait_send()

            @pl.when(sends_near)
            def _():
                near(which, h).wait_send()
    weight_send().wait_send()
    for n in range(len(chunks)):
        out_send(n).wait()


def shards(queries, keys, values, segments, out_weight):
    rows = queries.shape[0]
    assert 2 * rows == ATTENTION_SPAN
    heads = keys.shape[1] // HEAD_SIZE
    query_heads = queries.shape[1] // HEAD_SIZE
    group = query_heads // heads
    width = out_weight.shape[1]
    half = width // 2
    pieces = len(column_chunks(half))
    seg = segments.reshape(segments.shape[0] // rows, 1, rows)
    dma = pltpu.SemaphoreType.DMA
    anywhere = pl.BlockSpec(memory_space=pltpu.HBM)
    bf16 = jnp.bfloat16
    span = ATTENTION_SPAN + QUERY_TILE
    return pl.pallas_call(
        kernel,
        out_shape=pltpu.VMEM((rows, width), bf16),
        in_specs=[anywhere, anywhere, anywhere, pl.BlockSpec(memory_space=pltpu.VMEM), anywhere],
        out_specs=pl.BlockSpec(memory_space=pltpu.VMEM),
        scratch_shapes=[
            pltpu.VMEM((query_heads, rows, HEAD_SIZE), bf16),
            pltpu.VMEM((heads, 3 * rows, HEAD_SIZE), bf16),
            pltpu.VMEM((heads, 3 * rows, HEAD_SIZE), bf16),
            pltpu.VMEM((out_weight.shape[0], half), bf16),
            pltpu.VMEM((out_weight.shape[0], half), bf16),
            pltpu.VMEM((heads, rows, group * HEAD_SIZE), bf16),
            pltpu.VMEM((heads, rows, group * HEAD_SIZE), bf16),
            pltpu.VMEM((rows, half), jnp.float32),
            pltpu.VMEM((query_heads, rows, 2 * HEAD_SIZE), jnp.float32),
            pltpu.VMEM((query_heads, rows, HEAD_SIZE), jnp.float32),
            pltpu.VMEM((rows // QUERY_TILE, QUERY_TILE, span), jnp.float32),
            dma((query_heads,)), dma((2, heads)), dma, dma, dma,
            dma((2, heads)), dma((2, heads)), dma((2, heads)), dma((2, heads)),
            dma((heads,)), dma((heads,)), dma((pieces,)), dma((pieces,)),
        ],
        compiler_params=pltpu.CompilerParams(
            collective_id=0, has_side_effects=True, vmem_limit_bytes=55 * 1024 * 1024),
    )(queries, keys, values, seg, out_weight)


def solution(mesh):
    placed = (
        P(("groups", "seq"), "head"),
        P(("groups", "seq"), "head"),
        P(("groups", "seq"), "head"),
        P("groups"),
        P("head", None),
    )
    return jax.shard_map(
        shards, mesh=mesh, in_specs=placed, out_specs=P(("groups", "seq"), None), check_vma=False
    )
```

```python
import functools

import jax
import jax.numpy as jnp
from jax import lax
from jax.experimental import pallas as pl
from jax.experimental.pallas import tpu as pltpu
from jax.sharding import PartitionSpec as P

HEAD_SIZE = 128
SCALAR = 168
ATTENTION_SPAN = 1024
LOG2E = 1.4426950408889634
QUERY_TILE = 256
MESH = pl.DeviceIdType.MESH


def column_chunks(width):
    step = 768
    return [(at, min(step, width - at)) for at in range(0, width, step)]


def kernel(
    q_hbm, k_hbm, v_hbm, seg_ref, w_hbm, out_ref,
    q_s, k_s, v_s, w_own, w_peer, att_own, att_peer, acc, part, part_top, bias,
    q_sem, kv_sem, w_sem, ws_sem, wr_sem, zs_sem, zr_sem, ys_sem, yr_sem,
    as_sem, ar_sem, os_sem, or_sem,
):
    heads = k_s.shape[0]
    group = q_s.shape[0] // heads
    rows = q_s.shape[1]
    half = w_own.shape[1]
    seq = lax.axis_index("seq")
    core = lax.axis_index("head")
    peers = lax.axis_size("seq")
    odd = lax.rem(seq, 2)
    pair = seq + 1 - 2 * odd
    other = 1 - core
    chunks = column_chunks(half)

    def local_kv(which, h):
        src, dst = ((k_hbm, k_s), (v_hbm, v_s))[which]
        return pltpu.make_async_copy(
            src.at[:, pl.ds(h * HEAD_SIZE, HEAD_SIZE)],
            dst.at[h, pl.ds(2 * rows, rows), :], kv_sem.at[which, h])

    def local_q(n):
        return pltpu.make_async_copy(
            q_hbm.at[:, pl.ds(n * HEAD_SIZE, HEAD_SIZE)], q_s.at[n], q_sem.at[n])

    piece = rows // 2

    def far(which, h):
        src, dst = ((k_hbm, k_s), (v_hbm, v_s))[which // 2]
        return pltpu.make_async_remote_copy(
            src_ref=src.at[pl.ds(which % 2 * piece, piece), pl.ds(h * HEAD_SIZE, HEAD_SIZE)],
            dst_ref=dst.at[h, pl.ds(which % 2 * piece, piece), :],
            send_sem=zs_sem.at[which, h], recv_sem=zr_sem.at[which, h],
            device_id={"seq": seq + 2}, device_id_type=MESH)

    def near(which, h):
        src, dst = ((k_hbm, k_s), (v_hbm, v_s))[which // 2]
        return pltpu.make_async_remote_copy(
            src_ref=src.at[pl.ds(which % 2 * piece, piece), pl.ds(h * HEAD_SIZE, HEAD_SIZE)],
            dst_ref=dst.at[h, pl.ds(rows + which % 2 * piece, piece), :],
            send_sem=ys_sem.at[which, h], recv_sem=yr_sem.at[which, h],
            device_id={"seq": pair}, device_id_type=MESH)

    def relay(which, h):
        dst = (k_s, v_s)[which // 2]
        return pltpu.make_async_remote_copy(
            src_ref=dst.at[h, pl.ds(which % 2 * piece, piece), :],
            dst_ref=dst.at[h, pl.ds(rows + which % 2 * piece, piece), :],
            send_sem=ys_sem.at[which, h], recv_sem=yr_sem.at[which, h],
            device_id={"seq": pair}, device_id_type=MESH)

    def weight_send():
        return pltpu.make_async_remote_copy(
            src_ref=w_hbm.at[:, pl.ds(pl.multiple_of(other * half, HEAD_SIZE), half)],
            dst_ref=w_peer, send_sem=ws_sem, recv_sem=wr_sem,
            device_id={"head": other}, device_id_type=MESH)

    def weight_local():
        return pltpu.make_async_copy(
            w_hbm.at[:, pl.ds(pl.multiple_of(core * half, HEAD_SIZE), half)], w_own, w_sem)

    def attended_send(h):
        return pltpu.make_async_remote_copy(
            src_ref=att_own.at[h], dst_ref=att_peer.at[h],
            send_sem=as_sem.at[h], recv_sem=ar_sem.at[h],
            device_id={"head": other}, device_id_type=MESH)

    def out_view(n):
        at, width = chunks[n]
        return out_ref.at[:, pl.ds(pl.multiple_of(core * half + at, HEAD_SIZE), width)]

    def out_send(n):
        return pltpu.make_async_remote_copy(
            src_ref=out_view(n), dst_ref=out_view(n),
            send_sem=os_sem.at[n], recv_sem=or_sem.at[n],
            device_id={"head": other}, device_id_type=MESH)

    has_up = seq + 2 < peers
    has_down = seq >= 2
    even = odd == 0
    sends_near = jnp.logical_or(even, seq >= 3)
    relays = jnp.logical_and(jnp.logical_not(even), seq >= 3)
    gets_near = seq >= 1

    barrier = pltpu.get_barrier_semaphore()
    pl.semaphore_signal(barrier, inc=1, device_id={"head": other}, device_id_type=MESH)
    pl.semaphore_signal(barrier, inc=1, device_id={"seq": pair}, device_id_type=MESH)

    @pl.when(has_up)
    def _():
        pl.semaphore_signal(barrier, inc=1, device_id={"seq": seq + 2}, device_id_type=MESH)

    @pl.when(has_down)
    def _():
        pl.semaphore_signal(barrier, inc=1, device_id={"seq": seq - 2}, device_id_type=MESH)

    pl.semaphore_wait(
        barrier, 2 + jnp.minimum(peers - 1 - seq, 2) // 2 + jnp.minimum(seq, 2) // 2)

    for h in range(heads):
        for which in range(4):
            @pl.when(has_up)
            def _():
                far(which, h).start()

            @pl.when(even)
            def _():
                near(which, h).start()

    for h in range(heads):
        for which in range(2):
            local_kv(which, h).start()
        for g in range(group):
            local_q(h * group + g).start()
    weight_send().start()
    weight_local().start()

    @pl.when(jnp.logical_not(has_down))
    def _():
        k_s[:, 0:rows, :] = jnp.zeros((heads, rows, HEAD_SIZE), k_s.dtype)
        v_s[:, 0:rows, :] = jnp.zeros((heads, rows, HEAD_SIZE), v_s.dtype)

    @pl.when(jnp.logical_not(gets_near))
    def _():
        k_s[:, rows:2 * rows, :] = jnp.zeros((heads, rows, HEAD_SIZE), k_s.dtype)
        v_s[:, rows:2 * rows, :] = jnp.zeros((heads, rows, HEAD_SIZE), v_s.dtype)

    tile = QUERY_TILE
    span = ATTENTION_SPAN + tile
    seg_own = seg_ref[seq]
    seg_all = jnp.concatenate(
        [seg_ref[jnp.maximum(seq - 2, 0)], seg_ref[jnp.maximum(seq - 1, 0)], seg_own], axis=1)
    for b in range(rows // tile):
        seg_key = seg_all[:, b * tile:b * tile + span]
        for strip in range(tile // 128):
            lo = b * tile + strip * 128
            seg_query = jnp.broadcast_to(
                seg_own[:, lo:lo + 128].astype(jnp.float32), (128, 128)).T[:, :1]
            r = strip * 128 + lax.broadcasted_iota(jnp.int32, (128, span), 0)
            c = lax.broadcasted_iota(jnp.int32, (128, span), 1)
            position = seq * rows - ATTENTION_SPAN + b * tile + c
            allowed = (
                (c <= r + ATTENTION_SPAN) & (c > r) & (position >= 0)
                & (seg_key.astype(jnp.float32) == seg_query)
            )
            bias[b, strip * 128:(strip + 1) * 128, :] = jnp.where(allowed, 0.0, -1e30)

    factor = SCALAR ** (-0.5) * LOG2E
    halo = 2 * rows

    def with_ones(value):
        return jnp.concatenate([value, jnp.ones(value.shape, value.dtype)], axis=1)

    def score(query, key, added):
        return lax.dot_general(
            query, key, (((1,), (1,)), ((), ())), preferred_element_type=jnp.float32) + added

    def product(h, at, width):
        top = pl.ds(pl.multiple_of(h * (group * HEAD_SIZE), group * HEAD_SIZE), group * HEAD_SIZE)
        left = jnp.concatenate([att_own[h], att_peer[h]], axis=1)
        right = jnp.concatenate(
            [w_own[top, at:at + width], w_peer[top, at:at + width]], axis=0)
        return jnp.dot(left, right, preferred_element_type=jnp.float32)

    def inner_step(h, carry):
        for which in range(2):
            local_kv(which, h).wait()
        for g in range(group):
            local_q(h * group + g).wait()
        for b in range(rows // tile):
            inside = (b + 1) * tile
            key = k_s[h, halo:halo + inside, :]
            value = with_ones(v_s[h, halo:halo + inside, :])
            for g in range(group):
                n = h * group + g
                scores = score(
                    q_s[n, b * tile:(b + 1) * tile, :], key, bias[b, :, halo - b * tile:])
                top = jnp.max(scores, axis=1, keepdims=True)
                weights = jnp.exp2((scores - top) * factor).astype(jnp.bfloat16)
                part[n, b * tile:(b + 1) * tile, :] = jnp.dot(
                    weights, value, preferred_element_type=jnp.float32)
                part_top[n, b * tile:(b + 1) * tile, :] = jnp.broadcast_to(
                    top, (tile, HEAD_SIZE))
        return carry

    lax.fori_loop(0, heads, inner_step, 0)
    acc[...] = jnp.zeros_like(acc)

    def step(h, carry):
        for which in range(4):
            @pl.when(has_down)
            def _():
                far(which, h).wait_recv()

            @pl.when(relays)
            def _():
                relay(which, h).start()

        @pl.when(h == 1)
        def _():
            weight_local().wait()
            weight_send().wait_recv()

        @pl.when(h >= 1)
        def _():
            attended_send(h - 1).wait_recv()
            for at, width in chunks:
                acc[:, at:at + width] += product(h - 1, at, width)

        for which in range(4):
            @pl.when(gets_near)
            def _():
                near(which, h).wait_recv()

        for b in range(rows // tile):
            key = k_s[h, b * tile:halo, :]
            value = with_ones(v_s[h, b * tile:halo, :])
            for g in range(group):
                n = h * group + g
                scores = score(
                    q_s[n, b * tile:(b + 1) * tile, :], key, bias[b, :, :halo - b * tile])
                before = part_top[n, b * tile:(b + 1) * tile, :]
                top = jnp.maximum(jnp.max(scores, axis=1, keepdims=True), before[:, :1])
                weights = jnp.exp2((scores - top) * factor).astype(jnp.bfloat16)
                faded = jnp.exp2((before - top) * factor)
                mix = part[n, b * tile:(b + 1) * tile, :] * jnp.concatenate(
                    [faded, faded], axis=1) + jnp.dot(
                        weights, value, preferred_element_type=jnp.float32)
                att_own[h, b * tile:(b + 1) * tile, g * HEAD_SIZE:(g + 1) * HEAD_SIZE] = (
                    mix[:, :HEAD_SIZE] / mix[:, HEAD_SIZE:]).astype(jnp.bfloat16)
        attended_send(h).start()
        return carry

    lax.fori_loop(0, heads, step, 0)

    attended_send(heads - 1).wait_recv()
    for n, (at, width) in enumerate(chunks):
        out_view(n)[...] = (
            acc[:, at:at + width] + product(heads - 1, at, width)).astype(jnp.bfloat16)
        out_send(n).start()

    for h in range(heads):
        attended_send(h).wait_send()
        for which in range(4):
            @pl.when(has_up)
            def _():
                far(which, h).wait_send()

            @pl.when(sends_near)
            def _():
                near(which, h).wait_send()
    weight_send().wait_send()
    for n in range(len(chunks)):
        out_send(n).wait()


def shards(queries, keys, values, segments, out_weight):
    rows = queries.shape[0]
    assert 2 * rows == ATTENTION_SPAN
    heads = keys.shape[1] // HEAD_SIZE
    query_heads = queries.shape[1] // HEAD_SIZE
    group = query_heads // heads
    width = out_weight.shape[1]
    half = width // 2
    pieces = len(column_chunks(half))
    seg = segments.reshape(segments.shape[0] // rows, 1, rows)
    dma = pltpu.SemaphoreType.DMA
    anywhere = pl.BlockSpec(memory_space=pltpu.HBM)
    bf16 = jnp.bfloat16
    span = ATTENTION_SPAN + QUERY_TILE
    return pl.pallas_call(
        kernel,
        out_shape=pltpu.VMEM((rows, width), bf16),
        in_specs=[anywhere, anywhere, anywhere, pl.BlockSpec(memory_space=pltpu.VMEM), anywhere],
        out_specs=pl.BlockSpec(memory_space=pltpu.VMEM),
        scratch_shapes=[
            pltpu.VMEM((query_heads, rows, HEAD_SIZE), bf16),
            pltpu.VMEM((heads, 3 * rows, HEAD_SIZE), bf16),
            pltpu.VMEM((heads, 3 * rows, HEAD_SIZE), bf16),
            pltpu.VMEM((out_weight.shape[0], half), bf16),
            pltpu.VMEM((out_weight.shape[0], half), bf16),
            pltpu.VMEM((heads, rows, group * HEAD_SIZE), bf16),
            pltpu.VMEM((heads, rows, group * HEAD_SIZE), bf16),
            pltpu.VMEM((rows, half), jnp.float32),
            pltpu.VMEM((query_heads, rows, 2 * HEAD_SIZE), jnp.float32),
            pltpu.VMEM((query_heads, rows, HEAD_SIZE), jnp.float32),
            pltpu.VMEM((rows // QUERY_TILE, QUERY_TILE, span), jnp.float32),
            dma((query_heads,)), dma((2, heads)), dma, dma, dma,
            dma((4, heads)), dma((4, heads)), dma((4, heads)), dma((4, heads)),
            dma((heads,)), dma((heads,)), dma((pieces,)), dma((pieces,)),
        ],
        compiler_params=pltpu.CompilerParams(
            collective_id=0, has_side_effects=True, vmem_limit_bytes=55 * 1024 * 1024),
    )(queries, keys, values, seg, out_weight)


def solution(mesh):
    placed = (
        P(("groups", "seq"), "head"),
        P(("groups", "seq"), "head"),
        P(("groups", "seq"), "head"),
        P("groups"),
        P("head", None),
    )
    return jax.shard_map(
        shards, mesh=mesh, in_specs=placed, out_specs=P(("groups", "seq"), None), check_vma=False
    )
```
